256 devices in a mesh: fsdp: 32 (over z_lo, x, core), seq: 8 (over y, z_hi).
Axes of the slice: x: 4, y: 4, z: 8 (z_hi: 2, z_lo: 4; z = z_hi * 4 + z_lo), core: 2. Of those that a mesh axis runs over, the one named last changes fastest.
Arguments:
- queries: bfloat16 [32768, 3072], P(('fsdp', 'seq')), may hold values from -1000 to 1000
- keys: bfloat16 [32768, 3072], P(('fsdp', 'seq')), may hold values from -1000 to 1000
- values: bfloat16 [32768, 3072], P(('fsdp', 'seq')), may hold values from -6 to 6
- image_ids: int32 [32, 1024], P('fsdp'), may hold values from 0 to 15, never falling along the last dimension, each value on 1 to 512 neighbouring positions
- q_gain: float32 [128], replicated, may hold values from 0.6 to 6
- k_gain: float32 [128], replicated, may hold values from 0.6 to 6
- w_out: bfloat16 [3072, 6144], P('fsdp', 'seq'), may hold values from -0.109375 to 0.109375
- grad_y: bfloat16 [32768, 6144], P('fsdp', 'seq'), may hold values from -6 to 6
Outputs:
- grad_queries: bfloat16 [32768, 24, 128], P('fsdp', 'seq')
- grad_keys: bfloat16 [32768, 24, 128], P('fsdp', 'seq')
- grad_values: bfloat16 [32768, 24, 128], P('fsdp', 'seq')
- grad_w: float32 [3072, 6144], P('fsdp', 'seq')
The draws below stay inside these ranges and needn't reach their ends.
All inputs are finite; a program needn't handle non-finite values.
Results may differ from the reference program's by a relative error of at most 0.02.
The reference program's roundings to bfloat16 on the way count: a program that leaves them out, or rounds other values in their place, can miss the bound.
Values may be sent and summed in bfloat16 or wider, within the bound.
A program may use at most 128 MiB of HBM per device.

```python
import math
import jax
import jax.numpy as jnp
import numpy as np
from jax import lax

D = 6144
HEADS = 24
HEAD_DIM = 128
IMAGES = 16
SEQ_LEN = 1024
GROUPS = 32
TOKENS = 32768
N_SEQ = 8


def pair_fields(key):
    base = jax.random.fold_in(key, 101)
    parts = jax.random.split(base, 6)
    width = HEADS * HEAD_DIM
    span = math.log(10.0)
    col_q = jnp.exp(jax.random.uniform(parts[0], (1, width), minval=0.0, maxval=span))
    col_k = jnp.exp(jax.random.uniform(parts[1], (1, width), minval=0.0, maxval=span))
    row_q = jnp.exp(jax.random.uniform(parts[2], (TOKENS, 1), minval=0.0, maxval=span))
    row_k = jnp.exp(jax.random.uniform(parts[3], (TOKENS, 1), minval=0.0, maxval=span))
    raw_q = jnp.clip(jax.random.normal(parts[4], (TOKENS, width)), -6.0, 6.0)
    raw_k = jnp.clip(jax.random.normal(parts[5], (TOKENS, width)), -6.0, 6.0)
    keys_out = raw_k * col_k * row_k
    queries_out = raw_q * col_q * row_q
    return (queries_out, keys_out)


def draw_queries(key, part):
    return pair_fields(key)[0].astype(jnp.bfloat16)


def draw_keys(key, part):
    return pair_fields(key)[1].astype(jnp.bfloat16)


def draw_q_gain(key, part):
    inner = jax.random.fold_in(key, 202)
    return jax.random.uniform(inner, (HEAD_DIM,), minval=0.6, maxval=1.8)


def draw_k_gain(key, part):
    inner = jax.random.fold_in(key, 303)
    return jax.random.uniform(inner, (HEAD_DIM,), minval=0.6, maxval=1.8)


def steps_of(rng, shape, cuts, least, high):
    def one(dim, blocks):
        draws = jax.random.uniform(jax.random.fold_in(jax.random.fold_in(rng, 6), dim), (blocks,), jnp.float32, least / len(cuts), high / len(cuts))
        return jnp.repeat(jnp.exp(draws), shape[dim] // blocks).reshape((-1,) + (1,) * (len(shape) - dim - 1))

    level = one(*cuts[0])
    for cut in cuts[1:]:
        level = level * one(*cut)
    return level


def length_profile(amount, total, reach, lean):
    weights = [(1 << 20) // math.isqrt(grade ** lean) + 1 for grade in range(2, amount + 1)]
    surplus, counts = total - reach - (amount - 1), [1] * (amount - 1)
    while surplus > 0:
        movable = [i for i in range(amount - 1) if counts[i] < reach]
        whole, remaining = sum([weights[i] for i in movable]), surplus
        for i in movable:
            addition = min(reach - counts[i], max(1, remaining * weights[i] // whole), surplus)
            counts[i] = counts[i] + addition
            surplus = surplus - addition
    return np.array([reach] + counts)


def ragged(stream_key, count, total, most, lean):
    if count == 2:
        one = jax.random.randint(stream_key, (), max(1, total - most), min(most, total - 1) + 1)
        return jnp.stack([one, total - one])
    sizes = jnp.asarray(length_profile(count, total, most, lean), jnp.int32)
    twos = (count - 1) // 2
    donor, taker = sizes[1:1 + 2 * twos:2], sizes[2:2 + 2 * twos:2]
    slack = jnp.minimum(donor - 1, most - taker)
    shifted = jax.random.randint(jax.random.fold_in(stream_key, 1), (twos,), 0, 1 << 20) % (slack + 1)
    sizes = sizes.at[1:1 + 2 * twos:2].set(donor - shifted).at[2:2 + 2 * twos:2].set(taker + shifted)
    return sizes[jax.random.permutation(jax.random.fold_in(stream_key, 2), count)]


def normal_values(rng, dims, scale, most, cuts=(), dtype=jnp.bfloat16):
    array = jax.random.normal(rng, dims, jnp.float32) * scale
    if len(cuts) > 0:
        array = steps_of(rng, dims, cuts, -0.22, 0.18) * array
    return jnp.clip(array, min=-most, max=most).astype(dtype)


def setup_inputs(seed: int = 0) -> dict:
    streams_of = jax.random.split(jax.random.key(seed), 9)
    queries = draw_queries(jax.random.fold_in(streams_of[8], 71), 0)
    keys = draw_keys(jax.random.fold_in(streams_of[8], 71), 0)
    values = normal_values(streams_of[2], (TOKENS, HEADS * HEAD_DIM), 1.0, 6.0, ((0, 256),))
    image_ids = jax.vmap(lambda own: jnp.searchsorted(jnp.cumsum(ragged(own, IMAGES, SEQ_LEN, SEQ_LEN // 2, 2)), jnp.arange(SEQ_LEN), side="right"))(jax.random.split(streams_of[3], GROUPS)).reshape((GROUPS, SEQ_LEN)).astype(jnp.int32)
    q_gain = draw_q_gain(jax.random.fold_in(streams_of[8], 71), 0)
    k_gain = draw_k_gain(jax.random.fold_in(streams_of[8], 71), 0)
    w_out = normal_values(streams_of[6], (HEADS * HEAD_DIM, D), (HEADS * HEAD_DIM) ** -0.5, 0.109375, ((0, 32), (1, 8)))
    grad_y = normal_values(streams_of[7], (TOKENS, D), 1.0, 6.0, ((0, 32), (1, 8)))
    return {"queries": queries, "keys": keys, "values": values, "image_ids": image_ids, "q_gain": q_gain, "k_gain": k_gain, "w_out": w_out, "grad_y": grad_y}


def norm_parts(source, gain):
    wide = source.astype(jnp.float32)
    centred = wide - lax.optimization_barrier(jnp.mean(wide, axis=-1, keepdims=True))
    scale_inv = lax.rsqrt(lax.optimization_barrier(jnp.mean(centred * centred, axis=-1, keepdims=True)) + 1e-06)
    x_hat = centred * scale_inv
    return (x_hat, scale_inv, (x_hat * gain).astype(jnp.bfloat16))

def norm_back(grad_n, x_hat, scale_inv, gain):
    scaled = grad_n * gain
    return scale_inv * (scaled - lax.optimization_barrier(jnp.mean(scaled, axis=-1, keepdims=True)) - x_hat * lax.optimization_barrier(jnp.mean(scaled * x_hat, axis=-1, keepdims=True)))

def reference(queries, keys, values, image_ids, q_gain, k_gain, w_out, grad_y):
    scale_factor = HEAD_DIM ** (-0.5)
    width = D // N_SEQ
    grad_sum = jnp.zeros((TOKENS, HEADS * HEAD_DIM), jnp.float32)
    for column in range(N_SEQ):
        block = jnp.dot(grad_y[:, column * width:(column + 1) * width], w_out[:, column * width:(column + 1) * width].T, preferred_element_type=jnp.float32)
        block = lax.optimization_barrier(block.astype(jnp.bfloat16))
        grad_sum = grad_sum + block.astype(jnp.float32)
    attention_gradient = grad_sum.astype(jnp.bfloat16)

    def shaped(source):
        return source.reshape(GROUPS, SEQ_LEN, HEADS, HEAD_DIM).transpose(0, 2, 1, 3)

    def group_pass(packed):
        q_group, k_group, v_group, d_group, image_row = packed
        same_image = image_row[:, None] == image_row[None, :]

        def head_pass(inner):
            q_head, k_head, v_head, d_head = inner
            q_hat, q_inv, normalized_queries = norm_parts(q_head, q_gain)
            k_hat, k_inv, normalized_keys = norm_parts(k_head, k_gain)
            scores = jnp.dot(normalized_queries, normalized_keys.T, preferred_element_type=jnp.float32) * scale_factor
            scores = jnp.where(same_image, scores, -1e+30)
            row_top = lax.optimization_barrier(jnp.max(scores, axis=-1, keepdims=True))
            exp_terms = jnp.exp(scores - row_top)
            prob_rows = exp_terms / lax.optimization_barrier(jnp.sum(exp_terms, axis=-1, keepdims=True))
            probs_reduced_precision = prob_rows.astype(jnp.bfloat16)
            attended = jnp.dot(probs_reduced_precision, v_head, preferred_element_type=jnp.float32).astype(jnp.bfloat16)
            grad_v = jnp.dot(probs_reduced_precision.T, d_head, preferred_element_type=jnp.float32).astype(jnp.bfloat16)
            probability_gradient = jnp.dot(d_head, v_head.T, preferred_element_type=jnp.float32)
            row_delta = lax.optimization_barrier(jnp.sum(prob_rows * probability_gradient, axis=-1, keepdims=True))
            score_gradient = (prob_rows * (probability_gradient - row_delta) * scale_factor).astype(jnp.bfloat16)
            normed_query_gradient = jnp.dot(score_gradient, normalized_keys, preferred_element_type=jnp.float32)
            normed_key_gradient = jnp.dot(score_gradient.T, normalized_queries, preferred_element_type=jnp.float32)
            grad_q = norm_back(normed_query_gradient, q_hat, q_inv, q_gain).astype(jnp.bfloat16)
            grad_k = norm_back(normed_key_gradient, k_hat, k_inv, k_gain).astype(jnp.bfloat16)
            return (attended, grad_q, grad_k, grad_v)
        return lax.map(head_pass, (q_group, k_group, v_group, d_group))
    attended, grad_q, grad_k, grad_v = lax.map(group_pass, (shaped(queries), shaped(keys), shaped(values), shaped(attention_gradient), image_ids))

    def unshaped(source):
        return source.transpose(0, 2, 1, 3).reshape(TOKENS, HEADS, HEAD_DIM)
    attended_flat = unshaped(attended).reshape(TOKENS, HEADS * HEAD_DIM)
    grad_w = jnp.dot(attended_flat.T, grad_y, preferred_element_type=jnp.float32) * SEQ_LEN ** (-0.5)
    return (unshaped(grad_q), unshaped(grad_k), unshaped(grad_v), grad_w)
```

```python
import jax
import jax.numpy as jnp
from jax import lax
from jax.experimental import pallas as pl
from jax.experimental.pallas import tpu as pltpu
from jax.sharding import PartitionSpec as P

MESH = pl.DeviceIdType.MESH
F32 = jnp.float32
BF16 = jnp.bfloat16
HD = 128
HL = 3
HW = HL * HD
SEQ = 1024
TOK = 128
COLS = 768
CH = 256
NCH = SEQ // CH
SCALE = HD ** (-0.5)
W_SCALE = SEQ ** (-0.5)
SEGMENTS = (
    ((0, 96, 0, 0), (96, 32, 1, 0)),
    ((0, 64, 1, 32), (64, 64, 0, 96)),
    ((0, 32, 0, 160), (32, 96, 1, 96)),
)
N_QKV = 21


def nt(a, b):
    return lax.dot_general(a, b, (((1,), (1,)), ((), ())), preferred_element_type=F32)


def nn(a, b):
    return lax.dot_general(a, b, (((1,), (0,)), ((), ())), preferred_element_type=F32)


def stats(source):
    wide = source.astype(F32)
    centred = wide - jnp.mean(wide, axis=-1, keepdims=True)
    inv = lax.rsqrt(jnp.mean(centred * centred, axis=-1, keepdims=True) + 1e-06)
    return centred * inv, inv


def norm_back(grad_n, source, gain):
    x_hat, inv = stats(source)
    u = grad_n * gain
    return inv * (
        u
        - jnp.mean(u, axis=-1, keepdims=True)
        - x_hat * jnp.mean(u * x_hat, axis=-1, keepdims=True)
    )


def kernel(
    q_in, k_in, v_in, ids_row, ids_col, qgain, kgain, w_in, gy,
    gq, gk, gv, gw,
    qkv, qn, kn, knt, vt, gyo, wb, prob, pg, rsr, att, ga, dk, dv,
    acc, cbuf, crecv, xrecv, zsend, zrecv, fsend, frecv,
    s_own, s_qkv, r_qkv, s_w, r_w, s_gy, r_gy, s_rs, r_rs, s_at, r_at,
    s_c, r_c, s_x, r_x, s_z, r_z, s_f, r_f,
):
    f = lax.axis_index("fsdp")
    s = lax.axis_index("seq")
    zl, x, c = f // 8, (f // 2) % 4, f % 2
    y, zh = s // 2, s % 2
    oc = 1 - c
    ozh = 1 - zh
    xf = (x + 2) % 4
    xlo, xhi = x % 2, x // 2

    def dev(zl_=None, x_=None, c_=None, y_=None, zh_=None):
        zl_ = zl if zl_ is None else zl_
        x_ = x if x_ is None else x_
        c_ = c if c_ is None else c_
        y_ = y if y_ is None else y_
        zh_ = zh if zh_ is None else zh_
        return (zl_ * 8 + x_ * 2 + c_, y_ * 2 + zh_)

    def send(src, dst, ss, rs, where):
        return pltpu.make_async_remote_copy(
            src_ref=src, dst_ref=dst, send_sem=ss, recv_sem=rs,
            device_id=where, device_id_type=MESH,
        )

    offs = [(dy, 1) for dy in range(4)] + [(dy, 0) for dy in range(1, 4)]

    def seq_partner(dy, dz, sign=1):
        yy = (y + sign * dy + 4) % 4
        zz = (zh + dz) % 2
        return yy, zz

    barrier = pltpu.get_barrier_semaphore()
    partners = [dev(y_=a, zh_=b) for a, b in (seq_partner(dy, dz) for dy, dz in offs)]
    partners += [dev(x_=(x + o) % 4) for o in (1, 2, 3)]
    partners += [dev(zl_=(zl + o) % 4) for o in (1, 2, 3)]
    partners += [dev(c_=oc), dev(x_=xf, zh_=ozh)]
    for p in partners:
        pl.semaphore_signal(barrier, inc=1, device_id=p, device_id_type=MESH)
    pl.semaphore_wait(barrier, len(partners))

    same = xhi == zh
    w_own = wb.at[xhi, zl, xlo, c]
    w_swap = send(w_in, wb.at[1 - xhi, zl, xlo, c], s_w.at[0], r_w.at[0], dev(x_=xf, zh_=ozh))
    w_copy = pltpu.make_async_copy(w_in, w_own, s_own.at[3])

    @pl.when(same)
    def _():
        w_copy.start()

    @pl.when(jnp.logical_not(same))
    def _():
        w_swap.start()

    sources = (q_in, k_in, v_in)
    qkv_copies = []
    for i, (dy, dz) in enumerate(offs):
        yy, zz = seq_partner(dy, dz)
        ps = yy * 2 + zz
        cols = pl.ds(pl.multiple_of(ps * HW, 128), HW)
        rows = pl.ds(pl.multiple_of(s * TOK, TOK), TOK)
        for a in range(3):
            n = i * 3 + a
            qkv_copies.append(
                send(sources[a].at[:, cols], qkv.at[a, rows, :], s_qkv.at[n], r_qkv.at[n],
                     dev(y_=yy, zh_=zz))
            )
    own_copies = []
    for a in range(3):
        cols = pl.ds(pl.multiple_of(s * HW, 128), HW)
        rows = pl.ds(pl.multiple_of(s * TOK, TOK), TOK)
        own_copies.append(
            pltpu.make_async_copy(sources[a].at[:, cols], qkv.at[a, rows, :], s_own.at[a])
        )
    for cp in qkv_copies[12:]:
        cp.start()
    for cp in own_copies:
        cp.start()

    @pl.when(same)
    def _():
        w_copy.wait()

    @pl.when(jnp.logical_not(same))
    def _():
        w_swap.wait()

    wz = [
        send(w_own, w_own, s_w.at[o], r_w.at[o], dev(zl_=(zl + o) % 4)) for o in (1, 2, 3)
    ]
    for cp in wz:
        cp.start()
    for cp in qkv_copies[:12]:
        cp.start()
    for cp in wz:
        cp.wait()
    w_line = wb.at[xhi, :, xlo, c]
    wx = [
        send(w_line, w_line, s_w.at[3 + o], r_w.at[3 + o], dev(x_=(x + o) % 4))
        for o in (1, 2, 3)
    ]
    for cp in wx:
        cp.start()
    for cp in wx:
        cp.wait()
    wc = []
    for i in range(2):
        half = wb.at[i, :, :, c]
        wc.append(send(half, half, s_w.at[7 + i], r_w.at[7 + i], dev(c_=oc)))
    for cp in wc:
        cp.start()

    gy_copies = []
    for t in range(NCH):
        rows = pl.ds(t * CH, CH)
        gy_copies.append(
            send(gy.at[rows, :], gyo.at[rows, :], s_gy.at[t], r_gy.at[t], dev(zh_=ozh))
        )

    for cp in own_copies:
        cp.wait()
    for cp in qkv_copies:
        cp.wait_send()
    gy_copies[0].start()
    gy_copies[1].start()
    for cp in qkv_copies:
        cp.wait_recv()

    gain_q = qgain[...]
    gain_k = kgain[...]
    for h in range(HL):
        hc = pl.ds(h * HD, HD)

        def norm_step(t, carry, h=h, hc=hc):
            rows = pl.ds(pl.multiple_of(t * CH, CH), CH)
            qh, _ = stats(qkv[0, rows, hc])
            qn[rows, hc] = (qh * gain_q).astype(BF16)
            kh, _ = stats(qkv[1, rows, hc])
            knv = kh * gain_k
            kn[rows, hc] = knv.astype(BF16)
            knt[hc, rows] = knv.T.astype(BF16)
            vt[hc, rows] = qkv[2, rows, hc].astype(F32).T.astype(BF16)
            return carry

        lax.fori_loop(0, NCH, norm_step, 0)

    for h in range(HL):
        hc = pl.ds(h * HD, HD)

        def fwd_step(t, carry, h=h, hc=hc):
            rows = pl.ds(pl.multiple_of(t * CH, CH), CH)
            st = nt(kn[:, hc], qn[rows, hc]) * SCALE
            keep = ids_col[:, 0:1] == ids_row[:, rows]
            st = jnp.where(keep, st, -1e30)
            top = jnp.max(st, axis=0, keepdims=True)
            e = jnp.exp(st - top)
            total = jnp.sum(e, axis=0, keepdims=True)
            pt = e * (1.0 / total)
            prob[h, :, rows] = pt
            at = nn(vt[hc, :], pt.astype(BF16)).astype(BF16)
            for first, count, half, place in SEGMENTS[h]:
                at_rows = pl.ds(pl.multiple_of(y * 192 + place, 16), count)
                att[half, at_rows, rows] = at[first : first + count, :]
            return carry

        lax.fori_loop(0, NCH, fwd_step, 0)

    my_att = att.at[:, pl.ds(pl.multiple_of(y * 192, 16), 192), :]
    at_copies = [
        send(my_att, my_att, s_at.at[o - 1], r_at.at[o - 1], dev(y_=(y + o) % 4))
        for o in (1, 2, 3)
    ]
    for cp in at_copies:
        cp.start()
    for cp in wc:
        cp.wait()

    rs_copies = {}

    def grad_chunk(t):
        rows = pl.ds(t * CH, CH)
        gy_copies[t].wait()
        if t + 2 < NCH:
            gy_copies[t + 2].start()
        for o in (1, 2, 3, 0):
            yy = (y + o) % 4
            blk_own = wb[zh, yy].reshape(HW, COLS)
            blk_other = wb[ozh, yy].reshape(HW, COLS)
            val = nt(gy[rows, :], blk_own) + nt(gyo[rows, :], blk_other)
            pg[yy, rows, :] = val.astype(BF16)
            if o:
                cp = send(pg.at[yy, rows, :], rsr.at[o - 1, rows, :],
                          s_rs.at[t * 3 + o - 1], r_rs.at[t * 3 + o - 1], dev(y_=yy))
                rs_copies[(t, o)] = cp
                cp.start()

    def backward_chunk(t):
        rows = pl.ds(t * CH, CH)
        for o in (1, 2, 3):
            rs_copies[(t, o)].wait()
        total = pg[y, rows, :].astype(F32)
        for o in range(3):
            total = total + rsr[o, rows, :].astype(F32)
        ga[...] = total.astype(BF16)

        def head(h, carry):
            hc = pl.ds(pl.multiple_of(h * HD, HD), HD)
            do = ga[:, hc]
            dpt = nt(qkv[2, :, hc], do)
            pt = prob[h, :, rows]
            delta = jnp.sum(pt * dpt, axis=0, keepdims=True)
            dst = (pt * (dpt - delta) * SCALE).astype(BF16)
            dv_new = nn(pt.astype(BF16), do)
            dk_new = nn(dst, qn[rows, hc])
            if t == 0:
                dv[:, hc] = dv_new
                dk[:, hc] = dk_new
            else:
                dv[:, hc] += dv_new
                dk[:, hc] += dk_new
            dqt = nn(knt[hc, :], dst)
            gq[rows, hc] = norm_back(dqt.T, qkv[0, rows, hc], gain_q).astype(BF16)
            return carry

        lax.fori_loop(0, HL, head, 0)

    def weight_products(p):
        right = gy if p == 0 else gyo
        for half, mine in ((oc, False), (c, True)):
            def step(i, carry, half=half, mine=mine):
                a_rows = pl.ds(pl.multiple_of(i * 192, 64), 192)
                val = nn(att[half, a_rows, :], right[...]).reshape(4, 48, COLS)
                if mine:
                    acc[p, i] = val
                else:
                    cbuf[p, i] = val.astype(BF16)
                return carry

            lax.fori_loop(0, 4, step, 0)
            if not mine:
                core_copies[p].start()

    core_copies = [
        send(cbuf.at[p], crecv.at[p], s_c.at[p], r_c.at[p], dev(c_=oc)) for p in range(2)
    ]

    x_copies = {}

    def to_x(p):
        core_copies[p].wait()

        def step(i, carry):
            val = acc[p, i] + crecv[p, i].astype(F32)
            acc[p, i] = val
            cbuf[p, i] = val.astype(BF16)
            return carry

        lax.fori_loop(0, 4, step, 0)
        for o in (1, 2, 3):
            xx = (x + o) % 4
            quarter = (xx % 2) * 2 + xx // 2
            n = p * 3 + o - 1
            cp = send(cbuf.at[p, :, quarter], xrecv.at[p, o - 1], s_x.at[n], r_x.at[n],
                      dev(x_=xx))
            x_copies[(p, o)] = cp
            cp.start()

    z_copies = {}

    def to_z(p):
        for o in (1, 2, 3):
            x_copies[(p, o)].wait()
        quarter = xlo * 2 + xhi

        def step(i, carry):
            val = acc[p, i, quarter]
            for o in range(3):
                val = val + xrecv[p, o, i].astype(F32)
            acc[p, i, quarter] = val
            zsend[p, i] = val.astype(BF16)
            return carry

        lax.fori_loop(0, 4, step, 0)
        for o in (1, 2, 3):
            zz = (zl + o) % 4
            n = p * 3 + o - 1
            cp = send(zsend.at[p, zz], zrecv.at[p, o - 1], s_z.at[n], r_z.at[n], dev(zl_=zz))
            z_copies[(p, o)] = cp
            cp.start()

    def reduced(p):
        for o in (1, 2, 3):
            z_copies[(p, o)].wait()
        val = acc[p, zl, xlo * 2 + xhi]
        for o in range(3):
            val = val + zrecv[p, o].astype(F32)
        return val * W_SCALE

    mine_rows = pl.ds(pl.multiple_of(xhi * 48, 16), 48)
    other_rows = pl.ds(pl.multiple_of((1 - xhi) * 48, 16), 48)
    f_x = send(fsend.at[0], frecv.at[0], s_f.at[0], r_f.at[0], dev(x_=xf))
    f_z = send(fsend.at[1], frecv.at[1], s_f.at[1], r_f.at[1], dev(zh_=ozh))
    f_xz = send(fsend.at[1], frecv.at[2], s_f.at[2], r_f.at[2], dev(x_=xf, zh_=ozh))

    def finish_own():
        val = reduced(0)

        @pl.when(same)
        def _():
            gw[mine_rows, :] = val

        @pl.when(jnp.logical_not(same))
        def _():
            fsend[0] = val.astype(BF16)
            f_x.start()

    def finish_other():
        fsend[1] = reduced(1).astype(BF16)

        @pl.when(same)
        def _():
            f_z.start()
            f_x.wait_recv()
            gw[other_rows, :] = frecv[0].astype(F32)
            f_z.wait_send()

        @pl.when(jnp.logical_not(same))
        def _():
            f_xz.start()
            f_x.wait_send()
            f_z.wait_recv()
            gw[mine_rows, :] = frecv[1].astype(F32)
            f_xz.wait()
            gw[other_rows, :] = frecv[2].astype(F32)

    grad_chunk(0)
    grad_chunk(1)
    for cp in at_copies:
        cp.wait()
    weight_products(0)
    backward_chunk(0)
    to_x(0)
    grad_chunk(2)
    backward_chunk(1)
    to_z(0)
    grad_chunk(3)
    weight_products(1)
    to_x(1)
    finish_own()
    backward_chunk(2)
    to_z(1)
    backward_chunk(3)
    for h in range(HL):
        hc = pl.ds(h * HD, HD)

        def key_step(t, carry, hc=hc):
            rows = pl.ds(pl.multiple_of(t * CH, CH), CH)
            gk[rows, hc] = norm_back(dk[rows, hc], qkv[1, rows, hc], gain_k).astype(BF16)
            gv[rows, hc] = dv[rows, hc].astype(BF16)
            return carry

        lax.fori_loop(0, NCH, key_step, 0)
    finish_other()


def local(queries, keys, values, image_ids, q_gain, k_gain, w_out, grad_y):
    ids_col = jnp.broadcast_to(image_ids.reshape(SEQ, 1), (SEQ, 128))
    vm = pl.BlockSpec(memory_space=pltpu.VMEM)
    hb = pl.BlockSpec(memory_space=pl.ANY)
    dma = lambda n: pltpu.SemaphoreType.DMA((n,))
    vmem = pltpu.VMEM
    scratch = [
        vmem((3, SEQ, HW), BF16),
        vmem((SEQ, HW), BF16),
        vmem((SEQ, HW), BF16),
        vmem((HW, SEQ), BF16),
        vmem((HW, SEQ), BF16),
        vmem((SEQ, COLS), BF16),
        vmem((2, 4, 2, 2, 96, COLS), BF16),
        vmem((HL, SEQ, SEQ), F32),
        vmem((4, SEQ, HW), BF16),
        vmem((3, SEQ, HW), BF16),
        vmem((2, 768, SEQ), BF16),
        vmem((CH, HW), BF16),
        vmem((SEQ, HW), F32),
        vmem((SEQ, HW), F32),
        vmem((2, 4, 4, 48, COLS), F32),
        vmem((2, 4, 4, 48, COLS), BF16),
        vmem((2, 4, 4, 48, COLS), BF16),
        vmem((2, 3, 4, 48, COLS), BF16),
        vmem((2, 4, 48, COLS), BF16),
        vmem((2, 3, 48, COLS), BF16),
        vmem((2, 48, COLS), BF16),
        vmem((3, 48, COLS), BF16),
        dma(4),
        dma(N_QKV), dma(N_QKV),
        dma(9), dma(9),
        dma(NCH), dma(NCH),
        dma(3 * NCH), dma(3 * NCH),
        dma(3), dma(3),
        dma(2), dma(2),
        dma(6), dma(6),
        dma(6), dma(6),
        dma(3), dma(3),
    ]
    gq, gk, gv, gw = pl.pallas_call(
        kernel,
        out_shape=(
            jax.ShapeDtypeStruct((SEQ, HW), BF16),
            jax.ShapeDtypeStruct((SEQ, HW), BF16),
            jax.ShapeDtypeStruct((SEQ, HW), BF16),
            jax.ShapeDtypeStruct((96, COLS), F32),
        ),
        in_specs=[hb, hb, hb, vm, vm, vm, vm, vm, vm],
        out_specs=(vm, vm, vm, vm),
        scratch_shapes=scratch,
        compiler_params=pltpu.CompilerParams(
            collective_id=0, has_side_effects=True, vmem_limit_bytes=62 * 1024 * 1024
        ),
        name="attention_backward",
    )(
        queries, keys, values, image_ids, ids_col,
        q_gain.reshape(1, HD), k_gain.reshape(1, HD), w_out, grad_y,
    )
    heads = lambda a: a.reshape(SEQ, HL, HD)
    return heads(gq), heads(gk), heads(gv), gw


def solution(mesh):
    in_specs = (
        P(("fsdp", "seq"), None),
        P(("fsdp", "seq"), None),
        P(("fsdp", "seq"), None),
        P("fsdp", None),
        P(),
        P(),
        P("fsdp", "seq"),
        P("fsdp", "seq"),
    )
    out_specs = (
        P("fsdp", "seq", None),
        P("fsdp", "seq", None),
        P("fsdp", "seq", None),
        P("fsdp", "seq"),
    )
    return jax.shard_map(local, mesh=mesh, in_specs=in_specs, out_specs=out_specs, check_vma=False)
```

```python
import jax
import jax.numpy as jnp
from jax import lax
from jax.experimental import pallas as pl
from jax.experimental.pallas import tpu as pltpu
from jax.sharding import PartitionSpec as P

MESH = pl.DeviceIdType.MESH
F32 = jnp.float32
BF16 = jnp.bfloat16
HD = 128
HL = 3
HW = HL * HD
SEQ = 1024
TOK = 128
COLS = 768
CH = 256
NCH = SEQ // CH
SCALE = HD ** (-0.5)
W_SCALE = SEQ ** (-0.5)
SEGMENTS = (
    ((0, 96, 0, 0), (96, 32, 1, 0)),
    ((0, 64, 1, 32), (64, 64, 0, 96)),
    ((0, 32, 0, 160), (32, 96, 1, 96)),
)
N_QKV = 21
WIDTH = (COLS, COLS // 2, COLS // 2)
PHASES = len(WIDTH)


def nt(a, b):
    return lax.dot_general(a, b, (((1,), (1,)), ((), ())), preferred_element_type=F32)


def nn(a, b):
    return lax.dot_general(a, b, (((1,), (0,)), ((), ())), preferred_element_type=F32)


def stats(source):
    wide = source.astype(F32)
    centred = wide - jnp.mean(wide, axis=-1, keepdims=True)
    inv = lax.rsqrt(jnp.mean(centred * centred, axis=-1, keepdims=True) + 1e-06)
    return centred * inv, inv


def norm_back(grad_n, source, gain):
    x_hat, inv = stats(source)
    u = grad_n * gain
    return inv * (
        u
        - jnp.mean(u, axis=-1, keepdims=True)
        - x_hat * jnp.mean(u * x_hat, axis=-1, keepdims=True)
    )


def kernel(
    q_in, k_in, v_in, ids_row, ids_col, qgain, kgain, w_in, gy,
    gq, gk, gv, gw,
    qkv, qn, kn, knt, vt, gyo, wb, prob, pg, rsr, att, ga, dk, dv,
    *stage,
):
    acc, cbuf, crecv, xrecv, zsend, zrecv, fsend, frecv = (
        stage[PHASES * i : PHASES * (i + 1)] for i in range(8)
    )
    (
        s_own, s_qkv, r_qkv, s_w, r_w, s_gy, r_gy, s_rs, r_rs, s_at, r_at,
        s_c, r_c, s_x, r_x, s_z, r_z, s_f, r_f, line_sem,
    ) = stage[PHASES * 8 :]
    f = lax.axis_index("fsdp")
    s = lax.axis_index("seq")
    zl, x, c = f // 8, (f // 2) % 4, f % 2
    y, zh = s // 2, s % 2
    oc = 1 - c
    ozh = 1 - zh
    xf = (x + 2) % 4
    xlo, xhi = x % 2, x // 2

    def dev(zl_=None, x_=None, c_=None, y_=None, zh_=None):
        zl_ = zl if zl_ is None else zl_
        x_ = x if x_ is None else x_
        c_ = c if c_ is None else c_
        y_ = y if y_ is None else y_
        zh_ = zh if zh_ is None else zh_
        return (zl_ * 8 + x_ * 2 + c_, y_ * 2 + zh_)

    def send(src, dst, ss, rs, where):
        return pltpu.make_async_remote_copy(
            src_ref=src, dst_ref=dst, send_sem=ss, recv_sem=rs,
            device_id=where, device_id_type=MESH,
        )

    offs = [(dy, 1) for dy in range(4)] + [(dy, 0) for dy in range(1, 4)]

    def seq_partner(dy, dz, sign=1):
        yy = (y + sign * dy + 4) % 4
        zz = (zh + dz) % 2
        return yy, zz

    barrier = pltpu.get_barrier_semaphore()
    partners = [dev(y_=a, zh_=b) for a, b in (seq_partner(dy, dz) for dy, dz in offs)]
    partners += [dev(x_=(x + o) % 4) for o in (1, 2, 3)]
    partners += [dev(zl_=(zl + o) % 4) for o in (1, 2, 3)]
    partners += [dev(c_=oc), dev(x_=xf, zh_=ozh)]
    for p in partners:
        pl.semaphore_signal(barrier, inc=1, device_id=p, device_id_type=MESH)
    pl.semaphore_wait(barrier, len(partners))

    same = xhi == zh
    w_own = wb.at[xhi, zl, xlo, c]
    w_swap = send(w_in, wb.at[1 - xhi, zl, xlo, c], s_w.at[0], r_w.at[0], dev(x_=xf, zh_=ozh))
    w_copy = pltpu.make_async_copy(w_in, w_own, s_own.at[3])

    sources = (q_in, k_in, v_in)
    qkv_copies = []
    for i, (dy, dz) in enumerate(offs):
        yy, zz = seq_partner(dy, dz)
        ps = yy * 2 + zz
        cols = pl.ds(pl.multiple_of(ps * HW, 128), HW)
        rows = pl.ds(pl.multiple_of(s * TOK, TOK), TOK)
        for a in range(3):
            n = i * 3 + a
            qkv_copies.append(
                send(sources[a].at[:, cols], qkv.at[a, rows, :], s_qkv.at[n], r_qkv.at[n],
                     dev(y_=yy, zh_=zz))
            )
    own_copies = []
    for a in range(3):
        cols = pl.ds(pl.multiple_of(s * HW, 128), HW)
        rows = pl.ds(pl.multiple_of(s * TOK, TOK), TOK)
        own_copies.append(
            pltpu.make_async_copy(sources[a].at[:, cols], qkv.at[a, rows, :], s_own.at[a])
        )
    def start_exchange():
        @pl.when(same)
        def _():
            w_copy.start()

        @pl.when(jnp.logical_not(same))
        def _():
            w_swap.start()

        for cp in qkv_copies[12:]:
            cp.start()
        for cp in own_copies:
            cp.start()

    def swapped():
        @pl.when(same)
        def _():
            w_copy.wait()

        @pl.when(jnp.logical_not(same))
        def _():
            w_swap.wait()

    wz = [
        send(w_own, w_own, s_w.at[o], r_w.at[o], dev(zl_=(zl + o) % 4)) for o in (1, 2, 3)
    ]
    w_line = wb.at[xhi, :, xlo, c]
    wx = [
        send(w_line, w_line, s_w.at[3 + o], r_w.at[3 + o], dev(x_=(x + o) % 4))
        for o in (1, 2, 3)
    ]
    wc = []
    for i in range(2):
        half = wb.at[i, :, :, c]
        wc.append(send(half, half, s_w.at[7 + i], r_w.at[7 + i], dev(c_=oc)))

    def weights_line():
        for cp in wz:
            cp.start()

    def heads_across():
        for cp in qkv_copies[:12]:
            cp.start()

    def weights_cross():
        for cp in wz:
            cp.wait()
        for cp in wx:
            cp.start()

    def weights_plane():
        for cp in wx:
            cp.wait()
        for cp in wc:
            cp.start()

    left, right = pl.ds(0, COLS // 2), pl.ds(COLS // 2, COLS // 2)
    gy_left = []
    for t in range(2):
        part = (pl.ds(t * (SEQ // 2), SEQ // 2), left)
        gy_left.append(
            send(gy.at[part], gyo.at[part], s_gy.at[NCH + t], r_gy.at[NCH + t], dev(zh_=ozh))
        )
    gy_right = []
    for t in range(NCH):
        part = (pl.ds(t * CH, CH), right)
        gy_right.append(send(gy.at[part], gyo.at[part], s_gy.at[t], r_gy.at[t], dev(zh_=ozh)))

    def sent_heads():
        for cp in own_copies:
            cp.wait()
        for cp in qkv_copies:
            cp.wait_send()

    gy_all = gy_left + gy_right

    def send_grad_y(*which):
        for n in which:
            gy_all[n].start()

    def sent_grad_y(*which):
        for n in which:
            gy_all[n].wait_send()

    def got_heads():
        for cp in qkv_copies:
            cp.wait_recv()

    gain_q = qgain[...]
    gain_k = kgain[...]
    def norms(h):
        hc = pl.ds(h * HD, HD)

        def norm_step(t, carry):
            rows = pl.ds(pl.multiple_of(t * CH, CH), CH)
            qh, _ = stats(qkv[0, rows, hc])
            qn[rows, hc] = (qh * gain_q).astype(BF16)
            kh, _ = stats(qkv[1, rows, hc])
            knv = kh * gain_k
            kn[rows, hc] = knv.astype(BF16)
            knt[hc, rows] = knv.T.astype(BF16)
            vt[hc, rows] = qkv[2, rows, hc].astype(F32).T.astype(BF16)
            return carry

        lax.fori_loop(0, NCH, norm_step, 0)

    def line_signal():
        for o in (1, 2, 3):
            pl.semaphore_signal(
                line_sem, inc=1, device_id=dev(zl_=(zl + o) % 4), device_id_type=MESH
            )

    def line_wait():
        pl.semaphore_wait(line_sem, 3)

    def att_copy(t, o):
        tile = att.at[
            :,
            pl.ds(pl.multiple_of(y * 192, 16), 192),
            pl.ds(pl.multiple_of(t * CH, CH), CH),
        ]
        n = t * 3 + o - 1
        return send(tile, tile, s_at.at[n], r_at.at[n], dev(y_=(y + o) % 4))

    def forward():
        def fwd_step(t, carry):
            rows = pl.ds(pl.multiple_of(t * CH, CH), CH)
            keep = ids_col[:, 0:1] == ids_row[:, rows]
            for h in range(HL):
                hc = pl.ds(h * HD, HD)
                st = nt(kn[:, hc], qn[rows, hc]) * SCALE
                st = jnp.where(keep, st, -1e30)
                top = jnp.max(st, axis=0, keepdims=True)
                e = jnp.exp(st - top)
                total = jnp.sum(e, axis=0, keepdims=True)
                pt = e * (1.0 / total)
                prob[h, :, rows] = pt
                at = nn(vt[hc, :], pt.astype(BF16)).astype(BF16)
                for first, count, half, place in SEGMENTS[h]:
                    at_rows = pl.ds(pl.multiple_of(y * 192 + place, 16), count)
                    att[half, at_rows, rows] = at[first : first + count, :]
            for o in (1, 2, 3):
                att_copy(t, o).start()
            return carry

        lax.fori_loop(0, NCH, fwd_step, 0)

    def got_weights():
        for cp in wc:
            cp.wait()

    def got_attended():
        def step(t, carry):
            for o in (1, 2, 3):
                att_copy(t, o).wait()
            return carry

        lax.fori_loop(0, NCH, step, 0)

    rs_copies = {}

    def grad_chunk(t):
        rows = pl.ds(t * CH, CH)
        if t == 0:
            for cp in gy_left:
                cp.wait_recv()
        gy_right[t].wait_recv()
        for o in (1, 2, 3, 0):
            yy = (y + o) % 4
            blk_own = wb[zh, yy].reshape(HW, COLS)
            blk_other = wb[ozh, yy].reshape(HW, COLS)
            val = nt(gy[rows, :], blk_own) + nt(gyo[rows, :], blk_other)
            pg[yy, rows, :] = val.astype(BF16)
            if o:
                cp = send(pg.at[yy, rows, :], rsr.at[o - 1, rows, :],
                          s_rs.at[t * 3 + o - 1], r_rs.at[t * 3 + o - 1], dev(y_=yy))
                rs_copies[(t, o)] = cp
                cp.start()

    def backward_chunk(t):
        rows = pl.ds(t * CH, CH)
        for o in (1, 2, 3):
            rs_copies[(t, o)].wait()
        total = pg[y, rows, :].astype(F32)
        for o in range(3):
            total = total + rsr[o, rows, :].astype(F32)
        ga[...] = total.astype(BF16)

        def head(h, carry):
            hc = pl.ds(pl.multiple_of(h * HD, HD), HD)
            do = ga[:, hc]
            dpt = nt(qkv[2, :, hc], do)
            pt = prob[h, :, rows]
            delta = jnp.sum(pt * dpt, axis=0, keepdims=True)
            dst = (pt * (dpt - delta) * SCALE).astype(BF16)
            dv_new = nn(pt.astype(BF16), do)
            dk_new = nn(dst, qn[rows, hc])
            if t == 0:
                dv[:, hc] = dv_new
                dk[:, hc] = dk_new
            else:
                dv[:, hc] += dv_new
                dk[:, hc] += dk_new
            dqt = nn(knt[hc, :], dst)
            gq[h, rows, :] = norm_back(dqt.T, qkv[0, rows, hc], gain_q).astype(BF16)
            return carry

        lax.fori_loop(0, HL, head, 0)

    core_copies = [
        send(cbuf[p], crecv[p], s_c.at[p], r_c.at[p], dev(c_=oc)) for p in range(PHASES)
    ]

    def weight_products(p):
        wide = COLS // 2
        source, first = ((gy, 0), (gyo, 0), (gyo, wide))[p]
        for half, mine in ((oc, False), (c, True)):
            for n in range(WIDTH[p] // wide):
                val = nn(att[half], source[:, pl.ds(first + n * wide, wide)])
                val = val.reshape(4, 4, 48, wide)
                to = pl.ds(n * wide, wide)
                if mine:
                    acc[p][:, :, :, to] = val
                else:
                    cbuf[p][:, :, :, to] = val.astype(BF16)
            if not mine:
                core_copies[p].start()

    x_copies = {}

    def to_x(p):
        core_copies[p].wait()

        def step(i, carry):
            val = acc[p][i] + crecv[p][i].astype(F32)
            acc[p][i] = val
            cbuf[p][i] = val.astype(BF16)
            return carry

        lax.fori_loop(0, 4, step, 0)
        for o in (1, 2, 3):
            xx = (x + o) % 4
            quarter = (xx % 2) * 2 + xx // 2
            n = p * 3 + o - 1
            cp = send(cbuf[p].at[:, quarter], xrecv[p].at[o - 1], s_x.at[n], r_x.at[n],
                      dev(x_=xx))
            x_copies[(p, o)] = cp
            cp.start()

    z_copies = {}

    def to_z(p):
        for o in (1, 2, 3):
            x_copies[(p, o)].wait()
        quarter = xlo * 2 + xhi

        def step(i, carry):
            val = acc[p][i, quarter]
            for o in range(3):
                val = val + xrecv[p][o, i].astype(F32)
            acc[p][i, quarter] = val
            zsend[p][i] = val.astype(BF16)
            return carry

        lax.fori_loop(0, 4, step, 0)
        for o in (1, 2, 3):
            zz = (zl + o) % 4
            n = p * 3 + o - 1
            cp = send(zsend[p].at[zz], zrecv[p].at[o - 1], s_z.at[n], r_z.at[n], dev(zl_=zz))
            z_copies[(p, o)] = cp
            cp.start()

    def reduced(p):
        for o in (1, 2, 3):
            z_copies[(p, o)].wait()
        val = acc[p][zl, xlo * 2 + xhi]
        for o in range(3):
            val = val + zrecv[p][o].astype(F32)
        return val * W_SCALE

    mine_rows = pl.ds(pl.multiple_of(xhi * 48, 16), 48)
    other_rows = pl.ds(pl.multiple_of((1 - xhi) * 48, 16), 48)
    f_x = send(fsend[0], frecv[0].at[0], s_f.at[0], r_f.at[0], dev(x_=xf))
    f_z = [
        send(fsend[p], frecv[p].at[0], s_f.at[p], r_f.at[p], dev(zh_=ozh))
        for p in range(1, PHASES)
    ]
    f_xz = [
        send(fsend[p], frecv[p].at[1], s_f.at[2 + p], r_f.at[2 + p], dev(x_=xf, zh_=ozh))
        for p in range(1, PHASES)
    ]

    def finish(p):
        val = reduced(p)
        if p == 0:

            @pl.when(same)
            def _():
                gw[mine_rows, :] = val

            @pl.when(jnp.logical_not(same))
            def _():
                fsend[0][...] = val.astype(BF16)
                f_x.start()

        else:
            fsend[p][...] = val.astype(BF16)

            @pl.when(same)
            def _():
                f_z[p - 1].start()

            @pl.when(jnp.logical_not(same))
            def _():
                f_xz[p - 1].start()

    def collect():
        @pl.when(same)
        def _():
            f_x.wait_recv()
            gw[other_rows, :] = frecv[0][0].astype(F32)
            for cp in f_z:
                cp.wait_send()

        @pl.when(jnp.logical_not(same))
        def _():
            f_x.wait_send()
            for p in range(1, PHASES):
                to = pl.ds((p - 1) * (COLS // 2), COLS // 2)
                f_z[p - 1].wait_recv()
                gw[mine_rows, to] = frecv[p][0].astype(F32)
                f_xz[p - 1].wait()
                gw[other_rows, to] = frecv[p][1].astype(F32)

    def key_grads():
        for h in range(HL):
            hc = pl.ds(h * HD, HD)

            def key_step(t, carry, h=h, hc=hc):
                rows = pl.ds(pl.multiple_of(t * CH, CH), CH)
                gk[h, rows, :] = norm_back(dk[rows, hc], qkv[1, rows, hc], gain_k).astype(BF16)
                gv[h, rows, :] = dv[rows, hc].astype(BF16)
                return carry

            lax.fori_loop(0, NCH, key_step, 0)

    start_exchange()
    swapped()
    weights_line()
    heads_across()
    sent_heads()
    got_heads()
    weights_cross()
    line_signal()
    norms(0)
    line_wait()
    send_grad_y(0, 1, 2, 3, 4, 5)
    norms(1)
    norms(2)
    forward()
    weights_plane()
    got_weights()
    grad_chunk(0)
    grad_chunk(1)
    got_attended()
    weight_products(0)
    weight_products(1)
    grad_chunk(2)
    backward_chunk(0)
    to_x(0)
    to_x(1)
    grad_chunk(3)
    weight_products(2)
    backward_chunk(1)
    to_x(2)
    to_z(0)
    backward_chunk(2)
    to_z(1)
    backward_chunk(3)
    finish(0)
    to_z(2)
    finish(1)
    key_grads()
    finish(2)
    sent_grad_y(0, 1, 2, 3, 4, 5)
    collect()


def local(queries, keys, values, image_ids, q_gain, k_gain, w_out, grad_y):
    ids_col = jnp.broadcast_to(image_ids.reshape(SEQ, 1), (SEQ, 128))
    vm = pl.BlockSpec(memory_space=pltpu.VMEM)
    hb = pl.BlockSpec(memory_space=pl.ANY)
    dma = lambda n: pltpu.SemaphoreType.DMA((n,))
    vmem = pltpu.VMEM
    scratch = [
        vmem((3, SEQ, HW), BF16),
        vmem((SEQ, HW), BF16),
        vmem((SEQ, HW), BF16),
        vmem((HW, SEQ), BF16),
        vmem((HW, SEQ), BF16),
        vmem((SEQ, COLS), BF16),
        vmem((2, 4, 2, 2, 96, COLS), BF16),
        vmem((HL, SEQ, SEQ), F32),
        vmem((4, SEQ, HW), BF16),
        vmem((3, SEQ, HW), BF16),
        vmem((2, 768, SEQ), BF16),
        vmem((CH, HW), BF16),
        vmem((SEQ, HW), F32),
        vmem((SEQ, HW), F32),
        *[vmem((4, 4, 48, w), F32) for w in WIDTH],
        *[vmem((4, 4, 48, w), BF16) for w in WIDTH],
        *[vmem((4, 4, 48, w), BF16) for w in WIDTH],
        *[vmem((3, 4, 48, w), BF16) for w in WIDTH],
        *[vmem((4, 48, w), BF16) for w in WIDTH],
        *[vmem((3, 48, w), BF16) for w in WIDTH],
        *[vmem((48, w), BF16) for w in WIDTH],
        *[vmem((2, 48, w), BF16) for w in WIDTH],
        dma(4),
        dma(N_QKV), dma(N_QKV),
        dma(9), dma(9),
        dma(NCH + 2), dma(NCH + 2),
        dma(3 * NCH), dma(3 * NCH),
        dma(3 * NCH), dma(3 * NCH),
        dma(PHASES), dma(PHASES),
        dma(3 * PHASES), dma(3 * PHASES),
        dma(3 * PHASES), dma(3 * PHASES),
        dma(5), dma(5),
        pltpu.SemaphoreType.REGULAR,
    ]
    gq, gk, gv, gw = pl.pallas_call(
        kernel,
        out_shape=(
            jax.ShapeDtypeStruct((HL, SEQ, HD), BF16),
            jax.ShapeDtypeStruct((HL, SEQ, HD), BF16),
            jax.ShapeDtypeStruct((HL, SEQ, HD), BF16),
            jax.ShapeDtypeStruct((96, COLS), F32),
        ),
        in_specs=[hb, hb, hb, vm, vm, vm, vm, vm, vm],
        out_specs=(vm, vm, vm, vm),
        scratch_shapes=scratch,
        compiler_params=pltpu.CompilerParams(
            collective_id=0, has_side_effects=True, vmem_limit_bytes=62 * 1024 * 1024
        ),
        name="attention_backward",
    )(
        queries, keys, values, image_ids, ids_col,
        q_gain.reshape(1, HD), k_gain.reshape(1, HD), w_out, grad_y,
    )
    heads = lambda a: a.transpose(1, 0, 2)
    return heads(gq), heads(gk), heads(gv), gw


def solution(mesh):
    in_specs = (
        P(("fsdp", "seq"), None),
        P(("fsdp", "seq"), None),
        P(("fsdp", "seq"), None),
        P("fsdp", None),
        P(),
        P(),
        P("fsdp", "seq"),
        P("fsdp", "seq"),
    )
    out_specs = (
        P("fsdp", "seq", None),
        P("fsdp", "seq", None),
        P("fsdp", "seq", None),
        P("fsdp", "seq"),
    )
    return jax.shard_map(local, mesh=mesh, in_specs=in_specs, out_specs=out_specs, check_vma=False)
```

```python
import jax
import jax.numpy as jnp
from jax import lax
from jax.experimental import pallas as pl
from jax.experimental.pallas import tpu as pltpu
from jax.sharding import PartitionSpec as P

MESH = pl.DeviceIdType.MESH
F32 = jnp.float32
BF16 = jnp.bfloat16
HD = 128
HL = 3
HW = HL * HD
SEQ = 1024
TOK = 128
COLS = 768
CH = 256
NCH = SEQ // CH
SCALE = HD ** (-0.5)
W_SCALE = SEQ ** (-0.5)
SEGMENTS = (
    ((0, 96, 0, 0), (96, 32, 1, 0)),
    ((0, 64, 1, 32), (64, 64, 0, 96)),
    ((0, 32, 0, 160), (32, 96, 1, 96)),
)
N_QKV = 21
WIDTH = (COLS, COLS // 2, COLS // 2)
PHASES = len(WIDTH)


def nt(a, b):
    return lax.dot_general(a, b, (((1,), (1,)), ((), ())), preferred_element_type=F32)


def nn(a, b):
    return lax.dot_general(a, b, (((1,), (0,)), ((), ())), preferred_element_type=F32)


def stats(source):
    wide = source.astype(F32)
    centred = wide - jnp.mean(wide, axis=-1, keepdims=True)
    inv = lax.rsqrt(jnp.mean(centred * centred, axis=-1, keepdims=True) + 1e-06)
    return centred * inv, inv


def norm_back(grad_n, source, gain):
    x_hat, inv = stats(source)
    u = grad_n * gain
    return inv * (
        u
        - jnp.mean(u, axis=-1, keepdims=True)
        - x_hat * jnp.mean(u * x_hat, axis=-1, keepdims=True)
    )


def kernel(
    q_in, k_in, v_in, ids_row, qgain, kgain, w_in, gy,
    gq, gk, gv, gw,
    qkv, qn, kn, knt, vt, gyo, wb, prob, pg, rsr, att, ga, dk, dv,
    *stage,
):
    acc, cbuf, crecv, xrecv, zsend, zrecv, fsend, frecv = (
        stage[PHASES * i : PHASES * (i + 1)] for i in range(8)
    )
    (
        s_own, s_qkv, r_qkv, s_w, r_w, s_gy, r_gy, s_rs, r_rs, s_at, r_at,
        s_c, r_c, s_x, r_x, s_z, r_z, s_f, r_f, line_sem, ids_col,
    ) = stage[PHASES * 8 :]
    f = lax.axis_index("fsdp")
    s = lax.axis_index("seq")
    zl, x, c = f // 8, (f // 2) % 4, f % 2
    y, zh = s // 2, s % 2
    oc = 1 - c
    ozh = 1 - zh
    xf = (x + 2) % 4
    xlo, xhi = x % 2, x // 2

    def dev(zl_=None, x_=None, c_=None, y_=None, zh_=None):
        zl_ = zl if zl_ is None else zl_
        x_ = x if x_ is None else x_
        c_ = c if c_ is None else c_
        y_ = y if y_ is None else y_
        zh_ = zh if zh_ is None else zh_
        return (zl_ * 8 + x_ * 2 + c_, y_ * 2 + zh_)

    def send(src, dst, ss, rs, where):
        return pltpu.make_async_remote_copy(
            src_ref=src, dst_ref=dst, send_sem=ss, recv_sem=rs,
            device_id=where, device_id_type=MESH,
        )

    offs = [(dy, 1) for dy in range(4)] + [(dy, 0) for dy in range(1, 4)]

    def seq_partner(dy, dz, sign=1):
        yy = (y + sign * dy + 4) % 4
        zz = (zh + dz) % 2
        return yy, zz

    barrier = pltpu.get_barrier_semaphore()
    partners = [dev(y_=a, zh_=b) for a, b in (seq_partner(dy, dz) for dy, dz in offs)]
    partners += [dev(x_=(x + o) % 4) for o in (1, 2, 3)]
    partners += [dev(zl_=(zl + o) % 4) for o in (1, 2, 3)]
    partners += [dev(c_=oc), dev(x_=xf, zh_=ozh)]
    for p in partners:
        pl.semaphore_signal(barrier, inc=1, device_id=p, device_id_type=MESH)
    pl.semaphore_wait(barrier, len(partners))

    same = xhi == zh
    w_own = wb.at[xhi, zl, xlo, c]
    w_swap = send(w_in, wb.at[1 - xhi, zl, xlo, c], s_w.at[0], r_w.at[0], dev(x_=xf, zh_=ozh))
    w_copy = pltpu.make_async_copy(w_in, w_own, s_own.at[3])

    sources = (q_in, k_in, v_in)
    qkv_copies = []
    for i, (dy, dz) in enumerate(offs):
        yy, zz = seq_partner(dy, dz)
        ps = yy * 2 + zz
        cols = pl.ds(pl.multiple_of(ps * HW, 128), HW)
        rows = pl.ds(pl.multiple_of(s * TOK, TOK), TOK)
        for a in range(3):
            n = i * 3 + a
            qkv_copies.append(
                send(sources[a].at[:, cols], qkv.at[a, rows, :], s_qkv.at[n], r_qkv.at[n],
                     dev(y_=yy, zh_=zz))
            )
    own_copies = []
    for a in range(3):
        cols = pl.ds(pl.multiple_of(s * HW, 128), HW)
        rows = pl.ds(pl.multiple_of(s * TOK, TOK), TOK)
        own_copies.append(
            pltpu.make_async_copy(sources[a].at[:, cols], qkv.at[a, rows, :], s_own.at[a])
        )
    def start_exchange():
        @pl.when(same)
        def _():
            w_copy.start()

        @pl.when(jnp.logical_not(same))
        def _():
            w_swap.start()

        for cp in qkv_copies[12:]:
            cp.start()
        for cp in own_copies:
            cp.start()

    def swapped():
        @pl.when(same)
        def _():
            w_copy.wait()

        @pl.when(jnp.logical_not(same))
        def _():
            w_swap.wait()

    wz = [
        send(w_own, w_own, s_w.at[o], r_w.at[o], dev(zl_=(zl + o) % 4)) for o in (1, 2, 3)
    ]
    wx = []
    for j in range(4):
        shard = wb.at[xhi, (zl - j + 4) % 4, xlo, c]
        wx.append([
            send(shard, shard, s_w.at[6 + j * 3 + o - 1], r_w.at[6 + j * 3 + o - 1],
                 dev(x_=(x + o) % 4))
            for o in (1, 2, 3)
        ])
    wc = []
    for i in range(2):
        half = wb.at[i, :, :, c]
        wc.append(send(half, half, s_w.at[4 + i], r_w.at[4 + i], dev(c_=oc)))

    def weights_line():
        for cp in wz:
            cp.start()
        for cp in wx[0]:
            cp.start()

    def heads_across():
        for cp in qkv_copies[:12]:
            cp.start()

    def weights_cross():
        for j in range(1, 4):
            wz[j - 1].wait()
            for cp in wx[j]:
                cp.start()

    def weights_plane():
        for group in wx:
            for cp in group:
                cp.wait()
        for cp in wc:
            cp.start()

    left, right = pl.ds(0, COLS // 2), pl.ds(COLS // 2, COLS // 2)
    gy_left = []
    for t in range(2):
        part = (pl.ds(t * (SEQ // 2), SEQ // 2), left)
        gy_left.append(
            send(gy.at[part], gyo.at[part], s_gy.at[NCH + t], r_gy.at[NCH + t], dev(zh_=ozh))
        )
    gy_right = []
    for t in range(NCH):
        part = (pl.ds(t * CH, CH), right)
        gy_right.append(send(gy.at[part], gyo.at[part], s_gy.at[t], r_gy.at[t], dev(zh_=ozh)))

    def sent_heads():
        for cp in own_copies:
            cp.wait()
        for cp in qkv_copies:
            cp.wait_send()

    gy_all = gy_left + gy_right

    def send_grad_y(*which):
        for n in which:
            gy_all[n].start()

    def sent_grad_y(*which):
        for n in which:
            gy_all[n].wait_send()

    def got_heads():
        for cp in qkv_copies:
            cp.wait_recv()

    gain_q = qgain[...]
    gain_k = kgain[...]
    def image_columns():
        for t in range(SEQ // HD):
            part = pl.ds(t * HD, HD)
            ids = jnp.broadcast_to(ids_row[:, part].astype(F32), (HD, HD))
            ids_col[part, :] = ids.T

    def norms(h):
        hc = pl.ds(h * HD, HD)

        def norm_step(t, carry):
            rows = pl.ds(pl.multiple_of(t * CH, CH), CH)
            qh, _ = stats(qkv[0, rows, hc])
            qn[rows, hc] = (qh * gain_q).astype(BF16)
            kh, _ = stats(qkv[1, rows, hc])
            knv = kh * gain_k
            kn[rows, hc] = knv.astype(BF16)
            knt[hc, rows] = knv.T.astype(BF16)
            vt[hc, rows] = qkv[2, rows, hc].astype(F32).T.astype(BF16)
            return carry

        lax.fori_loop(0, NCH, norm_step, 0)

    def line_signal():
        for o in (1, 2, 3):
            pl.semaphore_signal(
                line_sem, inc=1, device_id=dev(zl_=(zl + o) % 4), device_id_type=MESH
            )

    def line_wait():
        pl.semaphore_wait(line_sem, 3)

    def att_copy(t, o):
        tile = att.at[
            :,
            pl.ds(pl.multiple_of(y * 192, 16), 192),
            pl.ds(pl.multiple_of(t * CH, CH), CH),
        ]
        n = t * 3 + o - 1
        return send(tile, tile, s_at.at[n], r_at.at[n], dev(y_=(y + o) % 4))

    def forward(first, last):
        def fwd_step(t, carry):
            rows = pl.ds(pl.multiple_of(t * CH, CH), CH)
            keep = ids_col[:, 0:1] == ids_row[:, rows].astype(F32)
            for h in range(HL):
                hc = pl.ds(h * HD, HD)
                st = nt(kn[:, hc], qn[rows, hc]) * SCALE
                st = jnp.where(keep, st, -1e30)
                top = jnp.max(st, axis=0, keepdims=True)
                e = jnp.exp(st - top)
                total = jnp.sum(e, axis=0, keepdims=True)
                pt = e * (1.0 / total)
                prob[h, :, rows] = pt
                at = nn(vt[hc, :], pt.astype(BF16)).astype(BF16)
                for first, count, half, place in SEGMENTS[h]:
                    at_rows = pl.ds(pl.multiple_of(y * 192 + place, 16), count)
                    att[half, at_rows, rows] = at[first : first + count, :]
            for o in (1, 2, 3):
                att_copy(t, o).start()
            return carry

        lax.fori_loop(first, last, fwd_step, 0)

    def got_weights():
        for cp in wc:
            cp.wait()

    def got_attended():
        def step(t, carry):
            for o in (1, 2, 3):
                att_copy(t, o).wait()
            return carry

        lax.fori_loop(0, NCH, step, 0)

    rs_copies = {}

    def got_left():
        for cp in gy_left:
            cp.wait_recv()

    def got_right(t):
        gy_right[t].wait_recv()

    def grad_chunk(t):
        rows = pl.ds(t * CH, CH)
        for o in (1, 2, 3, 0):
            yy = (y + o) % 4
            blk_own = wb[zh, yy].reshape(HW, COLS)
            blk_other = wb[ozh, yy].reshape(HW, COLS)
            val = nt(gy[rows, :], blk_own) + nt(gyo[rows, :], blk_other)
            pg[yy, rows, :] = val.astype(BF16)
            if o:
                cp = send(pg.at[yy, rows, :], rsr.at[o - 1, rows, :],
                          s_rs.at[t * 3 + o - 1], r_rs.at[t * 3 + o - 1], dev(y_=yy))
                rs_copies[(t, o)] = cp
                cp.start()

    def backward_chunk(t):
        rows = pl.ds(t * CH, CH)
        for o in (1, 2, 3):
            rs_copies[(t, o)].wait()
        total = pg[y, rows, :].astype(F32)
        for o in range(3):
            total = total + rsr[o, rows, :].astype(F32)
        ga[...] = total.astype(BF16)

        def head(h, carry):
            hc = pl.ds(pl.multiple_of(h * HD, HD), HD)
            do = ga[:, hc]
            dpt = nt(qkv[2, :, hc], do)
            pt = prob[h, :, rows]
            delta = jnp.sum(pt * dpt, axis=0, keepdims=True)
            dst = (pt * (dpt - delta) * SCALE).astype(BF16)
            dv_new = nn(pt.astype(BF16), do)
            dk_new = nn(dst, qn[rows, hc])
            if t == 0:
                dv[:, hc] = dv_new
                dk[:, hc] = dk_new
            else:
                dv[:, hc] += dv_new
                dk[:, hc] += dk_new
            dqt = nn(knt[hc, :], dst)
            gq[h, rows, :] = norm_back(dqt.T, qkv[0, rows, hc], gain_q).astype(BF16)
            return carry

        lax.fori_loop(0, HL, head, 0)

    core_copies = [
        send(cbuf[p], crecv[p], s_c.at[p], r_c.at[p], dev(c_=oc)) for p in range(PHASES)
    ]

    def weight_products(p):
        wide = COLS // 2
        source, first = ((gy, 0), (gyo, 0), (gyo, wide))[p]
        for half, mine in ((oc, False), (c, True)):
            for n in range(WIDTH[p] // wide):
                val = nn(att[half], source[:, pl.ds(first + n * wide, wide)])
                val = val.reshape(4, 4, 48, wide)
                to = pl.ds(n * wide, wide)
                if mine:
                    acc[p][:, :, :, to] = val
                else:
                    cbuf[p][:, :, :, to] = val.astype(BF16)
            if not mine:
                core_copies[p].start()

    x_copies = {}

    def to_x(p):
        core_copies[p].wait()

        def step(i, carry):
            val = acc[p][i] + crecv[p][i].astype(F32)
            acc[p][i] = val
            cbuf[p][i] = val.astype(BF16)
            return carry

        lax.fori_loop(0, 4, step, 0)
        for o in (1, 2, 3):
            xx = (x + o) % 4
            quarter = (xx % 2) * 2 + xx // 2
            n = p * 3 + o - 1
            cp = send(cbuf[p].at[:, quarter], xrecv[p].at[o - 1], s_x.at[n], r_x.at[n],
                      dev(x_=xx))
            x_copies[(p, o)] = cp
            cp.start()

    z_copies = {}

    def to_z(p):
        for o in (1, 2, 3):
            x_copies[(p, o)].wait()
        quarter = xlo * 2 + xhi

        def step(i, carry):
            val = acc[p][i, quarter]
            for o in range(3):
                val = val + xrecv[p][o, i].astype(F32)
            acc[p][i, quarter] = val
            zsend[p][i] = val.astype(BF16)
            return carry

        lax.fori_loop(0, 4, step, 0)
        for o in (1, 2, 3):
            zz = (zl + o) % 4
            n = p * 3 + o - 1
            cp = send(zsend[p].at[zz], zrecv[p].at[o - 1], s_z.at[n], r_z.at[n], dev(zl_=zz))
            z_copies[(p, o)] = cp
            cp.start()

    def reduced(p):
        for o in (1, 2, 3):
            z_copies[(p, o)].wait()
        val = acc[p][zl, xlo * 2 + xhi]
        for o in range(3):
            val = val + zrecv[p][o].astype(F32)
        return val * W_SCALE

    mine_rows = pl.ds(pl.multiple_of(xhi * 48, 16), 48)
    other_rows = pl.ds(pl.multiple_of((1 - xhi) * 48, 16), 48)
    f_x = send(fsend[0], frecv[0].at[0], s_f.at[0], r_f.at[0], dev(x_=xf))
    f_z = [
        send(fsend[p], frecv[p].at[0], s_f.at[p], r_f.at[p], dev(zh_=ozh))
        for p in range(1, PHASES)
    ]
    f_xz = [
        send(fsend[p], frecv[p].at[1], s_f.at[2 + p], r_f.at[2 + p], dev(x_=xf, zh_=ozh))
        for p in range(1, PHASES)
    ]

    def finish(p):
        val = reduced(p)
        if p == 0:

            @pl.when(same)
            def _():
                gw[mine_rows, :] = val

            @pl.when(jnp.logical_not(same))
            def _():
                fsend[0][...] = val.astype(BF16)
                f_x.start()

        else:
            fsend[p][...] = val.astype(BF16)

            @pl.when(same)
            def _():
                f_z[p - 1].start()

            @pl.when(jnp.logical_not(same))
            def _():
                f_xz[p - 1].start()

    def collect():
        @pl.when(same)
        def _():
            f_x.wait_recv()
            gw[other_rows, :] = frecv[0][0].astype(F32)
            for cp in f_z:
                cp.wait_send()

        @pl.when(jnp.logical_not(same))
        def _():
            f_x.wait_send()
            for p in range(1, PHASES):
                to = pl.ds((p - 1) * (COLS // 2), COLS // 2)
                f_z[p - 1].wait_recv()
                gw[mine_rows, to] = frecv[p][0].astype(F32)
                f_xz[p - 1].wait()
                gw[other_rows, to] = frecv[p][1].astype(F32)

    def key_grads():
        for h in range(HL):
            hc = pl.ds(h * HD, HD)

            def key_step(t, carry, h=h, hc=hc):
                rows = pl.ds(pl.multiple_of(t * CH, CH), CH)
                gk[h, rows, :] = norm_back(dk[rows, hc], qkv[1, rows, hc], gain_k).astype(BF16)
                gv[h, rows, :] = dv[rows, hc].astype(BF16)
                return carry

            lax.fori_loop(0, NCH, key_step, 0)

    start_exchange()
    heads_across()
    image_columns()
    sent_heads()
    send_grad_y(0)
    got_heads()
    swapped()
    weights_line()
    norms(0)
    norms(1)
    norms(2)
    forward(0, 3)
    weights_cross()
    line_signal()
    line_wait()
    send_grad_y(1, 2, 3, 4, 5)
    forward(3, 4)
    weights_plane()
    got_attended()
    weight_products(0)
    got_weights()
    got_left()
    weight_products(1)
    to_x(0)
    to_x(1)
    got_right(0)
    grad_chunk(0)
    got_right(1)
    grad_chunk(1)
    backward_chunk(0)
    got_right(2)
    grad_chunk(2)
    to_z(0)
    backward_chunk(1)
    got_right(3)
    weight_products(2)
    grad_chunk(3)
    to_x(2)
    backward_chunk(2)
    to_z(1)
    finish(0)
    backward_chunk(3)
    to_z(2)
    finish(1)
    key_grads()
    finish(2)
    sent_grad_y(0, 1, 2, 3, 4, 5)
    collect()


def local(queries, keys, values, image_ids, q_gain, k_gain, w_out, grad_y):
    vm = pl.BlockSpec(memory_space=pltpu.VMEM)
    hb = pl.BlockSpec(memory_space=pl.ANY)
    dma = lambda n: pltpu.SemaphoreType.DMA((n,))
    vmem = pltpu.VMEM
    scratch = [
        vmem((3, SEQ, HW), BF16),
        vmem((SEQ, HW), BF16),
        vmem((SEQ, HW), BF16),
        vmem((HW, SEQ), BF16),
        vmem((HW, SEQ), BF16),
        vmem((SEQ, COLS), BF16),
        vmem((2, 4, 2, 2, 96, COLS), BF16),
        vmem((HL, SEQ, SEQ), F32),
        vmem((4, SEQ, HW), BF16),
        vmem((3, SEQ, HW), BF16),
        vmem((2, 768, SEQ), BF16),
        vmem((CH, HW), BF16),
        vmem((SEQ, HW), F32),
        vmem((SEQ, HW), F32),
        *[vmem((4, 4, 48, w), F32) for w in WIDTH],
        *[vmem((4, 4, 48, w), BF16) for w in WIDTH],
        *[vmem((4, 4, 48, w), BF16) for w in WIDTH],
        *[vmem((3, 4, 48, w), BF16) for w in WIDTH],
        *[vmem((4, 48, w), BF16) for w in WIDTH],
        *[vmem((3, 48, w), BF16) for w in WIDTH],
        *[vmem((48, w), BF16) for w in WIDTH],
        *[vmem((2, 48, w), BF16) for w in WIDTH],
        dma(4),
        dma(N_QKV), dma(N_QKV),
        dma(18), dma(18),
        dma(NCH + 2), dma(NCH + 2),
        dma(3 * NCH), dma(3 * NCH),
        dma(3 * NCH), dma(3 * NCH),
        dma(PHASES), dma(PHASES),
        dma(3 * PHASES), dma(3 * PHASES),
        dma(3 * PHASES), dma(3 * PHASES),
        dma(5), dma(5),
        pltpu.SemaphoreType.REGULAR,
        vmem((SEQ, HD), F32),
    ]
    gq, gk, gv, gw = pl.pallas_call(
        kernel,
        out_shape=(
            jax.ShapeDtypeStruct((HL, SEQ, HD), BF16),
            jax.ShapeDtypeStruct((HL, SEQ, HD), BF16),
            jax.ShapeDtypeStruct((HL, SEQ, HD), BF16),
            jax.ShapeDtypeStruct((96, COLS), F32),
        ),
        in_specs=[hb, hb, hb, vm, vm, vm, vm, vm],
        out_specs=(vm, vm, vm, vm),
        scratch_shapes=scratch,
        compiler_params=pltpu.CompilerParams(
            collective_id=0, has_side_effects=True, vmem_limit_bytes=62 * 1024 * 1024
        ),
        name="attention_backward",
    )(
        queries, keys, values, image_ids,
        q_gain.reshape(1, HD), k_gain.reshape(1, HD), w_out, grad_y,
    )
    heads = lambda a: a.transpose(1, 0, 2)
    return heads(gq), heads(gk), heads(gv), gw


def solution(mesh):
    in_specs = (
        P(("fsdp", "seq"), None),
        P(("fsdp", "seq"), None),
        P(("fsdp", "seq"), None),
        P("fsdp", None),
        P(),
        P(),
        P("fsdp", "seq"),
        P("fsdp", "seq"),
    )
    out_specs = (
        P("fsdp", "seq", None),
        P("fsdp", "seq", None),
        P("fsdp", "seq", None),
        P("fsdp", "seq"),
    )
    return jax.shard_map(local, mesh=mesh, in_specs=in_specs, out_specs=out_specs, check_vma=False)
```

```python
import jax
import jax.numpy as jnp
from jax import lax
from jax.experimental import pallas as pl
from jax.experimental.pallas import tpu as pltpu
from jax.sharding import PartitionSpec as P

MESH = pl.DeviceIdType.MESH
F32 = jnp.float32
BF16 = jnp.bfloat16
HD = 128
HL = 3
HW = HL * HD
SEQ = 1024
TOK = 128
COLS = 768
CH = 256
NCH = SEQ // CH
SCALE = HD ** (-0.5)
W_SCALE = SEQ ** (-0.5)
SEGMENTS = (
    ((0, 96, 0, 0), (96, 32, 1, 0)),
    ((0, 64, 1, 32), (64, 64, 0, 96)),
    ((0, 32, 0, 160), (32, 96, 1, 96)),
)
N_QKV = 21
WIDTH = (COLS, COLS // 2, COLS // 2)
PHASES = len(WIDTH)


def nt(a, b):
    return lax.dot_general(a, b, (((1,), (1,)), ((), ())), preferred_element_type=F32)


def nn(a, b):
    return lax.dot_general(a, b, (((1,), (0,)), ((), ())), preferred_element_type=F32)


def stats(source):
    wide = source.astype(F32)
    centred = wide - jnp.mean(wide, axis=-1, keepdims=True)
    inv = lax.rsqrt(jnp.mean(centred * centred, axis=-1, keepdims=True) + 1e-06)
    return centred * inv, inv


def norm_back(grad_n, source, gain):
    x_hat, inv = stats(source)
    u = grad_n * gain
    return inv * (
        u
        - jnp.mean(u, axis=-1, keepdims=True)
        - x_hat * jnp.mean(u * x_hat, axis=-1, keepdims=True)
    )


def kernel(
    q_in, k_in, v_in, ids_row, qgain, kgain, w_in, gy,
    gq, gk, gv, gw,
    qkv, qn, kn, knt, vt, gyo, wb, prob, pg, rsr, att, ga, dk, dv,
    *stage,
):
    acc, cbuf, crecv, xrecv, zsend, zrecv, fsend, frecv = (
        stage[PHASES * i : PHASES * (i + 1)] for i in range(8)
    )
    (
        s_own, s_qkv, r_qkv, s_w, r_w, s_gy, r_gy, s_rs, r_rs, s_at, r_at,
        s_c, r_c, s_x, r_x, s_z, r_z, s_f, r_f, line_sem, ids_col,
    ) = stage[PHASES * 8 :]
    f = lax.axis_index("fsdp")
    s = lax.axis_index("seq")
    zl, x, c = f // 8, (f // 2) % 4, f % 2
    y, zh = s // 2, s % 2
    oc = 1 - c
    ozh = 1 - zh
    xf = (x + 2) % 4
    xlo, xhi = x % 2, x // 2

    def dev(zl_=None, x_=None, c_=None, y_=None, zh_=None):
        zl_ = zl if zl_ is None else zl_
        x_ = x if x_ is None else x_
        c_ = c if c_ is None else c_
        y_ = y if y_ is None else y_
        zh_ = zh if zh_ is None else zh_
        return (zl_ * 8 + x_ * 2 + c_, y_ * 2 + zh_)

    def send(src, dst, ss, rs, where):
        return pltpu.make_async_remote_copy(
            src_ref=src, dst_ref=dst, send_sem=ss, recv_sem=rs,
            device_id=where, device_id_type=MESH,
        )

    offs = [(dy, 1) for dy in range(4)] + [(dy, 0) for dy in range(1, 4)]

    def seq_partner(dy, dz, sign=1):
        yy = (y + sign * dy + 4) % 4
        zz = (zh + dz) % 2
        return yy, zz

    barrier = pltpu.get_barrier_semaphore()
    partners = [dev(y_=a, zh_=b) for a, b in (seq_partner(dy, dz) for dy, dz in offs)]
    partners += [dev(x_=(x + o) % 4) for o in (1, 2, 3)]
    partners += [dev(zl_=(zl + o) % 4) for o in (1, 2, 3)]
    partners += [dev(c_=oc), dev(x_=xf, zh_=ozh)]
    for p in partners:
        pl.semaphore_signal(barrier, inc=1, device_id=p, device_id_type=MESH)
    pl.semaphore_wait(barrier, len(partners))

    same = xhi == zh
    w_own = wb.at[xhi, zl, xlo, c]
    w_swap = send(w_in, wb.at[1 - xhi, zl, xlo, c], s_w.at[0], r_w.at[0], dev(x_=xf, zh_=ozh))
    w_copy = pltpu.make_async_copy(w_in, w_own, s_own.at[3])

    sources = (q_in, k_in, v_in)
    qkv_copies = []
    for i, (dy, dz) in enumerate(offs):
        yy, zz = seq_partner(dy, dz)
        ps = yy * 2 + zz
        cols = pl.ds(pl.multiple_of(ps * HW, 128), HW)
        rows = pl.ds(pl.multiple_of(s * TOK, TOK), TOK)
        for a in range(3):
            n = i * 3 + a
            qkv_copies.append(
                send(sources[a].at[:, cols], qkv.at[a, rows, :], s_qkv.at[n], r_qkv.at[n],
                     dev(y_=yy, zh_=zz))
            )
    own_copies = []
    for a in range(3):
        cols = pl.ds(pl.multiple_of(s * HW, 128), HW)
        rows = pl.ds(pl.multiple_of(s * TOK, TOK), TOK)
        own_copies.append(
            pltpu.make_async_copy(sources[a].at[:, cols], qkv.at[a, rows, :], s_own.at[a])
        )
    def start_exchange():
        @pl.when(same)
        def _():
            w_copy.start()

        @pl.when(jnp.logical_not(same))
        def _():
            w_swap.start()

        for cp in qkv_copies[12:]:
            cp.start()
        for cp in own_copies:
            cp.start()

    def swapped():
        @pl.when(same)
        def _():
            w_copy.wait()

        @pl.when(jnp.logical_not(same))
        def _():
            w_swap.wait()

    wz = [
        send(w_own, w_own, s_w.at[o], r_w.at[o], dev(zl_=(zl + o) % 4)) for o in (1, 2, 3)
    ]
    wx = []
    for j in range(4):
        shard = wb.at[xhi, (zl - j + 4) % 4, xlo, c]
        wx.append([
            send(shard, shard, s_w.at[6 + j * 3 + o - 1], r_w.at[6 + j * 3 + o - 1],
                 dev(x_=(x + o) % 4))
            for o in (1, 2, 3)
        ])
    wc = []
    for i in range(2):
        half = wb.at[i, :, :, c]
        wc.append(send(half, half, s_w.at[4 + i], r_w.at[4 + i], dev(c_=oc)))

    def weights_line():
        for cp in wz:
            cp.start()
        for cp in wx[0]:
            cp.start()

    def heads_across():
        for cp in qkv_copies[:12]:
            cp.start()

    def weights_cross():
        for j in range(1, 4):
            wz[j - 1].wait()
            for cp in wx[j]:
                cp.start()

    def weights_plane():
        for group in wx:
            for cp in group:
                cp.wait()
        for cp in wc:
            cp.start()

    left, right = pl.ds(0, COLS // 2), pl.ds(COLS // 2, COLS // 2)
    gy_left = []
    for t in range(2):
        part = (pl.ds(t * (SEQ // 2), SEQ // 2), left)
        gy_left.append(
            send(gy.at[part], gyo.at[part], s_gy.at[NCH + t], r_gy.at[NCH + t], dev(zh_=ozh))
        )
    gy_right = []
    for t in range(NCH):
        part = (pl.ds(t * CH, CH), right)
        gy_right.append(send(gy.at[part], gyo.at[part], s_gy.at[t], r_gy.at[t], dev(zh_=ozh)))

    def sent_heads():
        for cp in own_copies:
            cp.wait()
        for cp in qkv_copies:
            cp.wait_send()

    gy_all = gy_left + gy_right

    def send_grad_y(*which):
        for n in which:
            gy_all[n].start()

    def sent_grad_y(*which):
        for n in which:
            gy_all[n].wait_send()

    def got_heads():
        for cp in qkv_copies:
            cp.wait_recv()

    gain_q = qgain[...]
    gain_k = kgain[...]
    def image_columns():
        for t in range(SEQ // HD):
            part = pl.ds(t * HD, HD)
            ids = jnp.broadcast_to(ids_row[:, part].astype(F32), (HD, HD))
            ids_col[part, :] = ids.T

    def norms(h):
        hc = pl.ds(h * HD, HD)

        def norm_step(t, carry):
            rows = pl.ds(pl.multiple_of(t * CH, CH), CH)
            qh, _ = stats(qkv[0, rows, hc])
            qn[rows, hc] = (qh * gain_q).astype(BF16)
            kh, _ = stats(qkv[1, rows, hc])
            knv = kh * gain_k
            kn[rows, hc] = knv.astype(BF16)
            knt[hc, rows] = knv.T.astype(BF16)
            vt[hc, rows] = qkv[2, rows, hc].astype(F32).T.astype(BF16)
            return carry

        lax.fori_loop(0, NCH, norm_step, 0)

    def line_signal():
        for o in (1, 2, 3):
            pl.semaphore_signal(
                line_sem, inc=1, device_id=dev(zl_=(zl + o) % 4), device_id_type=MESH
            )

    def line_wait():
        pl.semaphore_wait(line_sem, 3)

    def att_copy(t, o):
        tile = att.at[
            :,
            pl.ds(pl.multiple_of(y * 192, 16), 192),
            pl.ds(pl.multiple_of(t * CH, CH), CH),
        ]
        n = t * 3 + o - 1
        return send(tile, tile, s_at.at[n], r_at.at[n], dev(y_=(y + o) % 4))

    def forward(first, last):
        def fwd_step(t, carry):
            rows = pl.ds(pl.multiple_of(t * CH, CH), CH)
            keep = ids_col[:, 0:1] == ids_row[:, rows].astype(F32)
            for h in range(HL):
                hc = pl.ds(h * HD, HD)
                st = nt(kn[:, hc], qn[rows, hc]) * SCALE
                st = jnp.where(keep, st, -1e30)
                top = jnp.max(st, axis=0, keepdims=True)
                e = jnp.exp(st - top)
                total = jnp.sum(e, axis=0, keepdims=True)
                pt = e * (1.0 / total)
                prob[h, :, rows] = pt
                at = nn(vt[hc, :], pt.astype(BF16)).astype(BF16)
                for first, count, half, place in SEGMENTS[h]:
                    at_rows = pl.ds(pl.multiple_of(y * 192 + place, 16), count)
                    att[half, at_rows, rows] = at[first : first + count, :]
            for o in (1, 2, 3):
                att_copy(t, o).start()
            return carry

        lax.fori_loop(first, last, fwd_step, 0)

    def got_weights():
        for cp in wc:
            cp.wait()

    def got_attended():
        def step(t, carry):
            for o in (1, 2, 3):
                att_copy(t, o).wait()
            return carry

        lax.fori_loop(0, NCH, step, 0)

    rs_copies = {}

    def got_left():
        for cp in gy_left:
            cp.wait_recv()

    def got_right(t):
        gy_right[t].wait_recv()

    def grad_chunk(t):
        rows = pl.ds(t * CH, CH)
        for o in (1, 2, 3, 0):
            yy = (y + o) % 4
            blk_own = wb[zh, yy].reshape(HW, COLS)
            blk_other = wb[ozh, yy].reshape(HW, COLS)
            val = nt(gy[rows, :], blk_own) + nt(gyo[rows, :], blk_other)
            pg[yy, rows, :] = val.astype(BF16)
            if o:
                cp = send(pg.at[yy, rows, :], rsr.at[o - 1, rows, :],
                          s_rs.at[t * 3 + o - 1], r_rs.at[t * 3 + o - 1], dev(y_=yy))
                rs_copies[(t, o)] = cp
                cp.start()

    def backward_chunk(t):
        rows = pl.ds(t * CH, CH)
        for o in (1, 2, 3):
            rs_copies[(t, o)].wait()
        total = pg[y, rows, :].astype(F32)
        for o in range(3):
            total = total + rsr[o, rows, :].astype(F32)
        ga[...] = total.astype(BF16)

        def head(h, carry):
            hc = pl.ds(pl.multiple_of(h * HD, HD), HD)
            do = ga[:, hc]
            dpt = nt(qkv[2, :, hc], do)
            pt = prob[h, :, rows]
            delta = jnp.sum(pt * dpt, axis=0, keepdims=True)
            dst = (pt * (dpt - delta) * SCALE).astype(BF16)
            dv_new = nn(pt.astype(BF16), do)
            dk_new = nn(dst, qn[rows, hc])
            if t == 0:
                dv[:, hc] = dv_new
                dk[:, hc] = dk_new
            else:
                dv[:, hc] += dv_new
                dk[:, hc] += dk_new
            dqt = nn(knt[hc, :], dst)
            gq[h, rows, :] = norm_back(dqt.T, qkv[0, rows, hc], gain_q).astype(BF16)
            return carry

        lax.fori_loop(0, HL, head, 0)

    core_copies = [
        send(cbuf[p], crecv[p], s_c.at[p], r_c.at[p], dev(c_=oc)) for p in range(PHASES)
    ]

    def weight_products(p):
        wide = COLS // 2
        source, first = ((gy, 0), (gyo, 0), (gyo, wide))[p]
        for half, mine in ((oc, False), (c, True)):
            for n in range(WIDTH[p] // wide):
                val = nn(att[half], source[:, pl.ds(first + n * wide, wide)])
                val = val.reshape(4, 4, 48, wide)
                to = pl.ds(n * wide, wide)
                if mine:
                    acc[p][:, :, :, to] = val
                else:
                    cbuf[p][:, :, :, to] = val.astype(BF16)
            if not mine:
                core_copies[p].start()

    x_copies = {}

    def to_x(p):
        core_copies[p].wait()

        def step(i, carry):
            val = acc[p][i] + crecv[p][i].astype(F32)
            acc[p][i] = val
            cbuf[p][i] = val.astype(BF16)
            return carry

        lax.fori_loop(0, 4, step, 0)
        for o in (1, 2, 3):
            xx = (x + o) % 4
            quarter = (xx % 2) * 2 + xx // 2
            n = p * 3 + o - 1
            cp = send(cbuf[p].at[:, quarter], xrecv[p].at[o - 1], s_x.at[n], r_x.at[n],
                      dev(x_=xx))
            x_copies[(p, o)] = cp
            cp.start()

    z_copies = {}

    def to_z(p):
        for o in (1, 2, 3):
            x_copies[(p, o)].wait()
        quarter = xlo * 2 + xhi

        def step(i, carry):
            val = acc[p][i, quarter]
            for o in range(3):
                val = val + xrecv[p][o, i].astype(F32)
            acc[p][i, quarter] = val
            zsend[p][i] = val.astype(BF16)
            return carry

        lax.fori_loop(0, 4, step, 0)
        for o in (1, 2, 3):
            zz = (zl + o) % 4
            n = p * 3 + o - 1
            cp = send(zsend[p].at[zz], zrecv[p].at[o - 1], s_z.at[n], r_z.at[n], dev(zl_=zz))
            z_copies[(p, o)] = cp
            cp.start()

    def reduced(p):
        for o in (1, 2, 3):
            z_copies[(p, o)].wait()
        val = acc[p][zl, xlo * 2 + xhi]
        for o in range(3):
            val = val + zrecv[p][o].astype(F32)
        return val * W_SCALE

    mine_rows = pl.ds(pl.multiple_of(xhi * 48, 16), 48)
    other_rows = pl.ds(pl.multiple_of((1 - xhi) * 48, 16), 48)
    f_x = send(fsend[0], frecv[0].at[0], s_f.at[0], r_f.at[0], dev(x_=xf))
    f_z = [
        send(fsend[p], frecv[p].at[0], s_f.at[p], r_f.at[p], dev(zh_=ozh))
        for p in range(1, PHASES)
    ]
    f_xz = [
        send(fsend[p], frecv[p].at[1], s_f.at[2 + p], r_f.at[2 + p], dev(x_=xf, zh_=ozh))
        for p in range(1, PHASES)
    ]

    def finish(p):
        val = reduced(p)
        if p == 0:

            @pl.when(same)
            def _():
                gw[mine_rows, :] = val

            @pl.when(jnp.logical_not(same))
            def _():
                fsend[0][...] = val.astype(BF16)
                f_x.start()

        else:
            fsend[p][...] = val.astype(BF16)

            @pl.when(same)
            def _():
                f_z[p - 1].start()

            @pl.when(jnp.logical_not(same))
            def _():
                f_xz[p - 1].start()

    def collect():
        @pl.when(same)
        def _():
            f_x.wait_recv()
            gw[other_rows, :] = frecv[0][0].astype(F32)
            for cp in f_z:
                cp.wait_send()

        @pl.when(jnp.logical_not(same))
        def _():
            f_x.wait_send()
            for p in range(1, PHASES):
                to = pl.ds((p - 1) * (COLS // 2), COLS // 2)
                f_z[p - 1].wait_recv()
                gw[mine_rows, to] = frecv[p][0].astype(F32)
                f_xz[p - 1].wait()
                gw[other_rows, to] = frecv[p][1].astype(F32)

    def key_grads():
        for h in range(HL):
            hc = pl.ds(h * HD, HD)

            def key_step(t, carry, h=h, hc=hc):
                rows = pl.ds(pl.multiple_of(t * CH, CH), CH)
                gk[h, rows, :] = norm_back(dk[rows, hc], qkv[1, rows, hc], gain_k).astype(BF16)
                gv[h, rows, :] = dv[rows, hc].astype(BF16)
                return carry

            lax.fori_loop(0, NCH, key_step, 0)

    start_exchange()
    heads_across()
    image_columns()
    swapped()
    weights_line()
    sent_heads()
    send_grad_y(0)
    got_heads()
    norms(0)
    norms(1)
    norms(2)
    forward(0, 2)
    weights_cross()
    line_signal()
    line_wait()
    send_grad_y(1, 2, 3, 4, 5)
    forward(2, 4)
    weights_plane()
    got_attended()
    weight_products(0)
    got_weights()
    got_left()
    weight_products(1)
    to_x(0)
    to_x(1)
    got_right(0)
    grad_chunk(0)
    got_right(1)
    grad_chunk(1)
    backward_chunk(0)
    got_right(2)
    grad_chunk(2)
    to_z(0)
    backward_chunk(1)
    got_right(3)
    weight_products(2)
    grad_chunk(3)
    to_x(2)
    backward_chunk(2)
    to_z(1)
    finish(0)
    to_z(2)
    backward_chunk(3)
    finish(1)
    finish(2)
    key_grads()
    sent_grad_y(0, 1, 2, 3, 4, 5)
    collect()


def local(queries, keys, values, image_ids, q_gain, k_gain, w_out, grad_y):
    vm = pl.BlockSpec(memory_space=pltpu.VMEM)
    hb = pl.BlockSpec(memory_space=pl.ANY)
    dma = lambda n: pltpu.SemaphoreType.DMA((n,))
    vmem = pltpu.VMEM
    scratch = [
        vmem((3, SEQ, HW), BF16),
        vmem((SEQ, HW), BF16),
        vmem((SEQ, HW), BF16),
        vmem((HW, SEQ), BF16),
        vmem((HW, SEQ), BF16),
        vmem((SEQ, COLS), BF16),
        vmem((2, 4, 2, 2, 96, COLS), BF16),
        vmem((HL, SEQ, SEQ), F32),
        vmem((4, SEQ, HW), BF16),
        vmem((3, SEQ, HW), BF16),
        vmem((2, 768, SEQ), BF16),
        vmem((CH, HW), BF16),
        vmem((SEQ, HW), F32),
        vmem((SEQ, HW), F32),
        *[vmem((4, 4, 48, w), F32) for w in WIDTH],
        *[vmem((4, 4, 48, w), BF16) for w in WIDTH],
        *[vmem((4, 4, 48, w), BF16) for w in WIDTH],
        *[vmem((3, 4, 48, w), BF16) for w in WIDTH],
        *[vmem((4, 48, w), BF16) for w in WIDTH],
        *[vmem((3, 48, w), BF16) for w in WIDTH],
        *[vmem((48, w), BF16) for w in WIDTH],
        *[vmem((2, 48, w), BF16) for w in WIDTH],
        dma(4),
        dma(N_QKV), dma(N_QKV),
        dma(18), dma(18),
        dma(NCH + 2), dma(NCH + 2),
        dma(3 * NCH), dma(3 * NCH),
        dma(3 * NCH), dma(3 * NCH),
        dma(PHASES), dma(PHASES),
        dma(3 * PHASES), dma(3 * PHASES),
        dma(3 * PHASES), dma(3 * PHASES),
        dma(5), dma(5),
        pltpu.SemaphoreType.REGULAR,
        vmem((SEQ, HD), F32),
    ]
    gq, gk, gv, gw = pl.pallas_call(
        kernel,
        out_shape=(
            jax.ShapeDtypeStruct((HL, SEQ, HD), BF16),
            jax.ShapeDtypeStruct((HL, SEQ, HD), BF16),
            jax.ShapeDtypeStruct((HL, SEQ, HD), BF16),
            jax.ShapeDtypeStruct((96, COLS), F32),
        ),
        in_specs=[hb, hb, hb, vm, vm, vm, vm, vm],
        out_specs=(vm, vm, vm, vm),
        scratch_shapes=scratch,
        compiler_params=pltpu.CompilerParams(
            collective_id=0, has_side_effects=True, vmem_limit_bytes=62 * 1024 * 1024
        ),
        name="attention_backward",
    )(
        queries, keys, values, image_ids,
        q_gain.reshape(1, HD), k_gain.reshape(1, HD), w_out, grad_y,
    )
    heads = lambda a: a.transpose(1, 0, 2)
    return heads(gq), heads(gk), heads(gv), gw


def solution(mesh):
    in_specs = (
        P(("fsdp", "seq"), None),
        P(("fsdp", "seq"), None),
        P(("fsdp", "seq"), None),
        P("fsdp", None),
        P(),
        P(),
        P("fsdp", "seq"),
        P("fsdp", "seq"),
    )
    out_specs = (
        P("fsdp", "seq", None),
        P("fsdp", "seq", None),
        P("fsdp", "seq", None),
        P("fsdp", "seq"),
    )
    return jax.shard_map(local, mesh=mesh, in_specs=in_specs, out_specs=out_specs, check_vma=False)
```
